768 devices in a mesh: dp: 32 (over x, y), expert: 24 (over z, core).
Axes of the slice: x: 4, y: 8, z: 12, core: 2. Of those that a mesh axis runs over, the one named last changes fastest.
Arguments:
- tokens: bfloat16 [98304, 2048], P(('dp', 'expert')), may hold values from -6 to 6
- routes: int32 [98304, 2], P(('dp', 'expert')), may hold values from 0 to 23, all different within a row; in each aligned block of 128 rows (0 to 127, 128 to 255, ...) at most 11 rows name the same one
- route_scores: float32 [98304, 2], P(('dp', 'expert')), may hold values from -4 to 4
- out_grad: bfloat16 [98304, 2048], P(('dp', 'expert')), may hold values from -6 to 6
- gate_up: bfloat16 [24, 2048, 1024], P('expert'), may hold values from -0.125 to 0.125
- down_weight: bfloat16 [24, 2048, 512], P('expert'), may hold values from -0.25 to 0.25
Outputs:
- mixed_out: bfloat16 [98304, 2048], P(('dp', 'expert'))
- token_grad: bfloat16 [98304, 2048], P(('dp', 'expert'))
- grad_gate_up: float32 [24, 2048, 1024], P('expert', 'dp')
- grad_down: float32 [24, 2048, 512], P('expert', 'dp')
The draws below stay inside these ranges and needn't reach their ends.
Inputs may be any that keep to these rules, and one draw needn't show every extreme that they name: `routes`: the 2 experts of a token differ. Among the 128 tokens of one device no expert is named more than 11 times, and in some device's tokens an expert is named exactly 11 times.
All inputs are finite; a program needn't handle non-finite values.
Results may differ from the reference program's by a relative error of at most 0.015.
Values may be sent and summed in bfloat16 or wider, within the bound.
A program may use at most 64 MiB of HBM per device.

```python
import math
import jax
import jax.numpy as jnp
import numpy as np
from jax import lax

D = 2048
H = 512
TOP = 2
TOK_DEV = 128
EXPERTS = 24
CAP = 11
TOKENS = 98304
N_DP = 32
N_EXPERT = 24


def steps_of(own_key, extent, split, least, top_value):
    gain, own = 1.0, jax.random.fold_in(own_key, 6)
    for dim, blocks in split:
        draws = jnp.exp(jax.random.uniform(jax.random.fold_in(own, dim), (blocks,), jnp.float32, least / len(split), top_value / len(split)))
        gain = gain * jnp.repeat(draws, extent[dim] // blocks).reshape([-1 if axis == dim else 1 for axis in range(len(extent))])
    return gain


def shared_out(rng, own, number, rows, amount, top, reach, slope):
    sequence = jax.random.permutation(rng, amount)
    packed, ordinary = load_shares(amount, rows * top, reach, slope, True), load_shares(amount, rows * top, reach, slope, False)
    places = jnp.arange(amount)

    def named(tallies, offset_by):
        used = int((tallies > 0).sum())
        fixed = max(1, used // 4)
        passed = fixed + (places - fixed + offset_by * (used - fixed)) % max(1, amount - fixed)
        return jnp.zeros((amount,), jnp.int32).at[sequence[jnp.where(places < fixed, places, passed)]].set(jnp.asarray(tallies, jnp.int32))

    tallies = jnp.where(number % 4 == 0, named(packed, number // 4), named(ordinary, number - number // 4 - 1))
    mixed = jax.random.permutation(jax.random.fold_in(own, 3), amount)
    source_of, taker = mixed[0:amount // 2 * 2:2], mixed[1:amount // 2 * 2:2]
    margin = jnp.minimum(tallies[source_of] - 1, reach - tallies[taker]) // 2
    margin = jnp.where((source_of == sequence[0]) | (taker == sequence[0]) | (tallies[taker] == 0), 0, jnp.maximum(margin, 0))
    passed = jax.random.randint(jax.random.fold_in(own, 4), (amount // 2,), 0, 1 << 20) % (margin + 1)
    tallies = tallies.at[source_of].add(-passed).at[taker].add(passed)
    items = jnp.searchsorted(jnp.cumsum(tallies), jnp.arange(rows * top), side="right").astype(jnp.int32)
    grid = items.reshape(top, rows).T
    grid = grid[jax.random.permutation(jax.random.fold_in(own, 1), rows)]
    offset_by = jax.random.randint(jax.random.fold_in(own, 2), (rows, 1), 0, top)
    return jnp.take_along_axis(grid, (jnp.arange(top)[None, :] + offset_by) % top, axis=1)


def load_shares(amount, total, bound, skew, full):
    portions = [(1 << 20) // math.isqrt(standing ** skew) + 1 for standing in range(1, amount + 1)]
    largest = bound if full else min(bound, max(-(-total // amount), total * portions[0] // sum(portions)))
    least = 1 if total - largest >= amount - 1 else 0
    counts, surplus = [largest] + [least] * (amount - 1), total - largest - least * (amount - 1)
    while surplus > 0:
        candidates = [i for i in range(1, amount) if counts[i] < largest] or [i for i in range(1, amount) if counts[i] < bound]
        mass, budget = sum([portions[i] for i in candidates]), surplus
        for i in candidates:
            addition = min(bound - counts[i], max(1, budget * portions[i] // mass), surplus)
            counts[i] = counts[i] + addition
            surplus = surplus - addition
    return np.array(counts)


def noise(stream_key, dims, scale, most, split=(), kind=jnp.bfloat16):
    level = steps_of(stream_key, dims, split, -0.22, 0.18) if split else 1.0
    result = jax.random.normal(stream_key, dims, jnp.float32) * scale * level
    return jnp.minimum(jnp.maximum(result, -most), most).astype(kind)


def setup_inputs(seed: int = 0) -> dict:
    key_of = jax.random.split(jax.random.key(seed), 7)
    tokens = noise(key_of[0], (TOKENS, D), 1.0, 6.0, ((0, 768),))
    routes_keys = jax.random.split(jax.random.fold_in(key_of[1], 1), TOKENS // TOK_DEV)
    routes_turns = jax.random.permutation(jax.random.fold_in(key_of[1], 3), TOKENS // TOK_DEV)
    routes = jax.vmap(lambda own, number: shared_out(jax.random.fold_in(key_of[1], 2), own, number, TOK_DEV, EXPERTS, TOP, CAP, 2))(routes_keys, routes_turns).reshape((TOKENS, TOP))
    route_scores = noise(key_of[2], (TOKENS, TOP), 1.0, 4.0, ((0, 768),), jnp.float32)
    out_grad = noise(key_of[3], (TOKENS, D), 1.0, 6.0, ((0, 768),))
    gate_up = noise(key_of[4], (EXPERTS, D, 2 * H), D ** -0.5, 0.125, ((0, 24),))
    down_weight = noise(key_of[5], (EXPERTS, D, H), H ** -0.5, 0.25, ((0, 24),))
    return dict(tokens=tokens, routes=routes, route_scores=route_scores, out_grad=out_grad, gate_up=gate_up, down_weight=down_weight)


def expert_pass(row_block, grad_block, w_in, w_out):
    hidden_units = w_out.shape[1]
    preact = jnp.dot(row_block, w_in, preferred_element_type=jnp.float32)
    gate_pre = preact[:, :hidden_units]
    up_pre = preact[:, hidden_units:]
    hidden = (jax.nn.silu(gate_pre) * up_pre).astype(jnp.bfloat16)
    produced = jnp.dot(hidden, w_out.T, preferred_element_type=jnp.float32).astype(jnp.bfloat16)
    hidden_grad = jnp.dot(grad_block, w_out, preferred_element_type=jnp.float32)
    sigmoid_gate = jax.nn.sigmoid(gate_pre)
    gate_grad = hidden_grad * up_pre * sigmoid_gate * (1.0 + gate_pre * (1.0 - sigmoid_gate))
    up_grad = hidden_grad * gate_pre * sigmoid_gate
    pre_grad = jnp.concatenate([gate_grad, up_grad], axis=1).astype(jnp.bfloat16)
    input_grad = jnp.dot(pre_grad, w_in.T, preferred_element_type=jnp.float32).astype(jnp.bfloat16)
    term_in = jnp.dot(row_block.T, pre_grad, preferred_element_type=jnp.float32)
    term_down = jnp.dot(grad_block.T, hidden, preferred_element_type=jnp.float32)
    return produced, input_grad, term_in, term_down


def reference(tokens, routes, route_scores, out_grad, gate_up, down_weight):
    group_tokens = TOK_DEV * N_EXPERT
    group_routes = group_tokens * TOP
    group_slots = N_EXPERT * CAP
    scores_exp = jnp.exp(route_scores)
    weights = scores_exp / jnp.sum(scores_exp, axis=1, keepdims=True)
    route_grad = (weights[:, :, None] * out_grad[:, None, :].astype(jnp.float32)).astype(jnp.bfloat16)

    def per_group(totals, group_data):
        total_in, total_down = totals
        tok_group, route_group, weight_group, grad_group = group_data
        flat_routes = route_group.reshape(group_routes)
        expert_ids = lax.broadcasted_iota(jnp.int32, (group_routes, EXPERTS), 1)
        chosen = (flat_routes[:, None] == expert_ids).astype(jnp.int32)
        position = jnp.sum((jnp.cumsum(chosen, axis=0) - chosen) * chosen, axis=1).astype(jnp.int32)
        slot_table = jnp.full((EXPERTS, group_slots), group_routes, jnp.int32)
        slot_table = slot_table.at[flat_routes, position].set(jnp.arange(group_routes, dtype=jnp.int32))
        zero_row = jnp.zeros((1, D), tok_group.dtype)
        rows_source = jnp.concatenate([jnp.repeat(tok_group, TOP, axis=0), zero_row], axis=0)
        grads_source = jnp.concatenate([grad_group.reshape(group_routes, D), zero_row], axis=0)
        row_blocks = rows_source[slot_table]
        grad_blocks = grads_source[slot_table]

        def per_expert(expert_item):
            return expert_pass(*expert_item)

        produced, input_grad, term_in, term_down = lax.map(per_expert, (row_blocks, grad_blocks, gate_up, down_weight))
        total_in = total_in + lax.optimization_barrier(term_in.astype(jnp.bfloat16)).astype(jnp.float32)
        total_down = total_down + lax.optimization_barrier(term_down.astype(jnp.bfloat16)).astype(jnp.float32)
        lookup = (flat_routes * group_slots + position).astype(jnp.int32)
        picked = produced.reshape(EXPERTS * group_slots, D)[lookup].astype(jnp.float32).reshape(group_tokens, TOP, D)
        mixed_group = jnp.sum(weight_group[:, :, None] * picked, axis=1).astype(jnp.bfloat16)
        back_grads = input_grad.reshape(EXPERTS * group_slots, D)[lookup].astype(jnp.float32).reshape(group_tokens, TOP, D)
        token_group = jnp.sum(back_grads, axis=1).astype(jnp.bfloat16)
        return (total_in, total_down), (mixed_group, token_group)

    start_totals = (jnp.zeros((EXPERTS, D, 2 * H), jnp.float32), jnp.zeros((EXPERTS, D, H), jnp.float32))
    group_inputs = (tokens.reshape(N_DP, group_tokens, D), routes.reshape(N_DP, group_tokens, TOP), weights.reshape(N_DP, group_tokens, TOP), route_grad.reshape(N_DP, group_tokens, TOP, D))
    totals, outputs = lax.scan(per_group, start_totals, group_inputs)
    mixed_out = outputs[0].reshape(TOKENS, D)
    token_grad = outputs[1].reshape(TOKENS, D)
    return mixed_out, token_grad, totals[0] / N_DP, totals[1] / N_DP
```

```python
import functools

import jax
import jax.numpy as jnp
from jax import lax
from jax.experimental import pallas as pl
from jax.experimental.pallas import tpu as pltpu
from jax.sharding import PartitionSpec as P

BF = jnp.bfloat16
F32 = jnp.float32
MESH = pl.DeviceIdType.MESH
NX, NY = 4, 8
LANES = 256
CHUNK = 256
VMEM = pl.BlockSpec(memory_space=pltpu.VMEM)
ANY = pl.BlockSpec(memory_space=pl.ANY)


def put(wide, j, pieces, value):
    rows = value.shape[0]
    for h in range(2):
        wide[h][pl.ds(j, rows, stride=pieces), :] = value[:, h * 128 : (h + 1) * 128]


def take(wide, j, pieces, rows):
    return jnp.concatenate([wide[h][pl.ds(j, rows, stride=pieces), :] for h in range(2)], axis=1)


def fill(wide, value):
    for h in range(2):
        wide[h][...] = value[:, h * 128 : (h + 1) * 128]


def whole(wide):
    return jnp.concatenate([wide[0][...], wide[1][...]], axis=1)


def dot(a, b, ca, cb):
    return lax.dot_general(a, b, (((ca,), (cb,)), ((), ())), preferred_element_type=F32)


def one_hots(routes, experts, cap):
    top, tokens = routes.shape
    ids = lax.broadcasted_iota(jnp.int32, (experts, tokens), 0)
    chosen = [(routes[k : k + 1, :] == ids).astype(F32) for k in range(top)]
    before = (
        lax.broadcasted_iota(jnp.int32, (tokens, tokens), 0)
        < lax.broadcasted_iota(jnp.int32, (tokens, tokens), 1)
    ).astype(F32)
    counts = dot(sum(chosen).astype(BF), before.astype(BF), 1, 0)
    slots = lax.broadcasted_iota(jnp.int32, (experts * cap, tokens), 0)
    hots = []
    for k in range(top):
        position = jnp.sum(chosen[k] * counts, axis=0, keepdims=True)
        slot = routes[k : k + 1, :] * cap + position.astype(jnp.int32)
        hots.append((slots == slot).astype(F32))
    return hots


def route_weights(scores):
    e = jnp.exp(scores)
    return e / jnp.sum(e, axis=0, keepdims=True)


def pre_kernel(experts, cap, routes_ref, scores_ref, tokens_ref, grads_ref, x_ref, g_ref, *wide):
    hot0, hot1 = one_hots(routes_ref[...], experts, cap)
    w = route_weights(scores_ref[...])
    slot_w = jnp.sum(hot0 * w[0:1, :] + hot1 * w[1:2, :], axis=1, keepdims=True)
    hot = (hot0 + hot1).astype(BF)
    slots = experts * cap
    pieces = tokens_ref.shape[1] // LANES
    for src, dst, scale in ((tokens_ref, x_ref, None), (grads_ref, g_ref, slot_w)):
        for j in range(pieces):
            part = dot(hot, src[:, j * LANES : (j + 1) * LANES], 1, 0)
            if scale is not None:
                part = part * scale
            put(wide, j, pieces, part)
        dst[...] = whole(wide).astype(BF)


def post_kernel(experts, cap, routes_ref, scores_ref, out_ref, grad_ref, mixed_ref, token_ref, *wide):
    hot0, hot1 = one_hots(routes_ref[...], experts, cap)
    w = route_weights(scores_ref[...])
    tokens = w.shape[1]
    cols = jnp.transpose(jnp.concatenate([w, jnp.zeros((6, tokens), F32)], axis=0))
    w0, w1 = cols[:, 0:1], cols[:, 1:2]
    both = (hot0 + hot1).astype(BF)
    hot0, hot1 = hot0.astype(BF), hot1.astype(BF)
    slots = experts * cap
    pieces = mixed_ref.shape[1] // LANES
    fill(wide, out_ref[...].astype(F32))
    for j in range(pieces):
        part = take(wide, j, pieces, slots).astype(BF)
        mixed_ref[:, j * LANES : (j + 1) * LANES] = (
            w0 * dot(hot0, part, 0, 0) + w1 * dot(hot1, part, 0, 0)
        ).astype(BF)
    fill(wide, grad_ref[...].astype(F32))
    for j in range(pieces):
        part = take(wide, j, pieces, slots).astype(BF)
        token_ref[:, j * LANES : (j + 1) * LANES] = dot(both, part, 0, 0).astype(BF)


def expert_kernel(
    experts, cap, sx, sg, win_hbm, wout_hbm, rp, rg2, ggu, gd,
    win, wout, rx, rg, wide0, wide1, x, g, pre, hid, pg, s2p, s2g,
    ga, ra, y1, ry, gb, rb, x1, rx2,
    wsem, lsem, xs, xr, gs, gr, ps, pr, qs, qr, as_, ar, ys, yr, bs, br, cs, cr,
):
    wide = (wide0, wide1)
    me = lax.axis_index("expert")
    dp = lax.axis_index("dp")
    mx, my = dp // NY, lax.rem(dp, NY)
    n = experts
    slots = experts * cap
    width = x.shape[1]
    pieces = width // LANES
    hidden = hid.shape[1]
    n_in = 2 * hidden // CHUNK
    n_x = ga.shape[0]

    def zdev(k):
        return {"expert": lax.rem(me + k, n)}

    def xdev(d):
        return {"dp": lax.rem(mx + d, NX) * NY + my}

    def ydev(d):
        return {"dp": mx * NY + lax.rem(my + d, NY)}

    def remote(src, dst, ssem, rsem, dev):
        return pltpu.make_async_remote_copy(
            src_ref=src, dst_ref=dst, send_sem=ssem, recv_sem=rsem, device_id=dev, device_id_type=MESH
        )

    barrier = pltpu.get_barrier_semaphore()

    @pl.loop(1, n)
    def _(k):
        pl.semaphore_signal(barrier, inc=1, device_id=zdev(k), device_id_type=MESH)

    for d in range(1, NX):
        pl.semaphore_signal(barrier, inc=1, device_id=xdev(d), device_id_type=MESH)
    for d in range(1, NY):
        pl.semaphore_signal(barrier, inc=1, device_id=ydev(d), device_id_type=MESH)
    pl.semaphore_wait(barrier, (n - 1) + (NX - 1) + (NY - 1))

    def dispatch(k, src, dst, ssem, rsem):
        return remote(src.at[lax.rem(me + k, n)], dst.at[k], ssem.at[k], rsem.at[k], zdev(k))

    def give_back(k, src, dst, ssem, rsem):
        return remote(src.at[k], dst.at[me], ssem.at[k], rsem.at[k], zdev(n - k))

    def start_all(make, *refs):
        @pl.loop(1, n // 2)
        def _(k):
            make(k, *refs).start()
            make(n - k, *refs).start()

        make(n // 2, *refs).start()

    def wait_sent(make, *refs):
        @pl.loop(1, n)
        def _(k):
            make(k, *refs).wait_send()

    start_all(dispatch, sx, rx, xs, xr)
    start_all(dispatch, sg, rg, gs, gr)
    own_x = pltpu.make_async_copy(sx.at[me], rx.at[0], lsem.at[0])
    own_g = pltpu.make_async_copy(sg.at[me], rg.at[0], lsem.at[1])
    own_x.start()
    own_g.start()
    load_in = pltpu.make_async_copy(win_hbm, win, wsem.at[0])
    load_out = pltpu.make_async_copy(wout_hbm, wout, wsem.at[1])
    load_in.start()
    load_out.start()

    def narrow(src, dst):
        fill(wide, src[...].reshape(slots * pieces, LANES).astype(F32))
        for j in range(pieces):
            dst[:, j * LANES : (j + 1) * LANES] = take(wide, j, pieces, slots).astype(BF)

    def widen(rows, weights, dst):
        for j in range(pieces):
            put(wide, j, pieces, dot(rows, weights[j * LANES : (j + 1) * LANES, :], 1, 1))
        dst[...] = whole(wide).astype(BF).reshape(n, cap * pieces, LANES)

    own_x.wait()
    load_in.wait()
    load_out.wait()

    @pl.loop(1, n)
    def _(k):
        dispatch(k, sx, rx, xs, xr).wait_recv()

    narrow(rx, x)

    for c in range(hidden // CHUNK):
        lo, hi = c * CHUNK, (c + 1) * CHUNK
        gate = dot(x[...], win[:, lo:hi], 1, 0)
        up = dot(x[...], win[:, hidden + lo : hidden + hi], 1, 0)
        pre[:, lo:hi] = gate
        pre[:, hidden + lo : hidden + hi] = up
        hid[:, lo:hi] = (gate * (1.0 / (1.0 + jnp.exp(-gate))) * up).astype(BF)
    widen(hid[...], wout, s2p)
    start_all(give_back, s2p, rp, ps, pr)
    home_p = pltpu.make_async_copy(s2p.at[0], rp.at[me], lsem.at[0])
    home_p.start()

    own_g.wait()

    @pl.loop(1, n)
    def _(k):
        dispatch(k, sg, rg, gs, gr).wait_recv()

    narrow(rg, g)
    for c in range(hidden // CHUNK):
        lo, hi = c * CHUNK, (c + 1) * CHUNK
        hg = dot(g[...], wout[:, lo:hi], 1, 0)
        gate = pre[:, lo:hi]
        up = pre[:, hidden + lo : hidden + hi]
        s = 1.0 / (1.0 + jnp.exp(-gate))
        pg[:, lo:hi] = (hg * up * s * (1.0 + gate * (1.0 - s))).astype(BF)
        pg[:, hidden + lo : hidden + hi] = (hg * gate * s).astype(BF)

    rows_x = width // NX
    rows_y = rows_x // NY

    def send_a(c, d):
        return remote(
            ga.at[c, lax.rem(mx + d, NX)], ra.at[c, d], as_.at[c, d], ar.at[c, d], xdev(d)
        )

    def send_b(d):
        return remote(gb.at[:, lax.rem(my + d, NY)], rb.at[d], bs.at[d], br.at[d], ydev(d))

    def send_y(c, d):
        return remote(y1.at[c, lax.rem(my + d, NY)], ry.at[c, d], ys.at[c, d], yr.at[c, d], ydev(d))

    def send_c(d):
        return remote(x1.at[lax.rem(mx + d, NX)], rx2.at[d], cs.at[d], cr.at[d], xdev(d))

    last = hidden - CHUNK
    gb[...] = dot(g[...], hid[:, last:hidden], 0, 0).astype(BF).reshape(NX, NY, rows_y, CHUNK)
    for d in (1, 7, 2, 6, 3, 5, 4):
        send_b(d).start()
    for c in range(n_x):
        lo = c * CHUNK
        if c < n_in:
            part = dot(x[...], pg[:, lo : lo + CHUNK], 0, 0)
        else:
            lo -= n_in * CHUNK
            part = dot(g[...], hid[:, lo : lo + CHUNK], 0, 0)
        ga[c] = part.astype(BF).reshape(NX, rows_x, CHUNK)
        for d in (1, 3, 2):
            send_a(c, d).start()

    widen(pg[...], win, s2g)
    start_all(give_back, s2g, rg2, qs, qr)
    home_g = pltpu.make_async_copy(s2g.at[0], rg2.at[me], lsem.at[1])
    home_g.start()

    def sum_x(c):
        for d in range(1, NX):
            send_a(c, d).wait_recv()
        total = ga[c, mx].astype(F32)
        for d in range(1, NX):
            total = total + ra[c, d].astype(F32)
        y1[c] = total.astype(BF).reshape(NY, rows_y, CHUNK)
        for d in (1, 7, 2, 6, 3, 5, 4):
            send_y(c, d).start()

    def sum_y():
        for d in range(1, NY):
            send_b(d).wait_recv()
        total = gb[:, my].astype(F32)
        for d in range(1, NY):
            total = total + rb[d].astype(F32)
        x1[...] = total.astype(BF)
        for d in (1, 3, 2):
            send_c(d).start()

    for c in range(n_x):
        sum_x(c)
        if c == 1:
            sum_y()

    groups = float(NX * NY)
    for c in range(n_x):
        for d in range(1, NY):
            send_y(c, d).wait_recv()
        total = y1[c, my].astype(F32)
        for d in range(1, NY):
            total = total + ry[c, d].astype(F32)
        lo = c * CHUNK
        if c < n_in:
            ggu[:, lo : lo + CHUNK] = total / groups
        else:
            lo -= n_in * CHUNK
            gd[:, lo : lo + CHUNK] = total / groups
    for d in range(1, NX):
        send_c(d).wait_recv()
    total = x1[mx].astype(F32)
    for d in range(1, NX):
        total = total + rx2[d].astype(F32)
    gd[:, last:hidden] = total / groups

    home_p.wait()
    home_g.wait()

    @pl.loop(1, n)
    def _(k):
        give_back(k, s2p, rp, ps, pr).wait_recv()
        give_back(k, s2g, rg2, qs, qr).wait_recv()

    wait_sent(dispatch, sx, rx, xs, xr)
    wait_sent(dispatch, sg, rg, gs, gr)
    wait_sent(give_back, s2p, rp, ps, pr)
    wait_sent(give_back, s2g, rg2, qs, qr)
    for d in range(1, NX):
        for c in range(n_x):
            send_a(c, d).wait_send()
        send_c(d).wait_send()
    for d in range(1, NY):
        for c in range(n_x):
            send_y(c, d).wait_send()
        send_b(d).wait_send()


def body(tokens, routes, route_scores, out_grad, gate_up, down_weight):
    n = lax.axis_size("expert")
    rows, width = tokens.shape
    top = routes.shape[1]
    hidden = down_weight.shape[2]
    cap = (rows * top + n - 1) // n
    slots = n * cap
    pieces = width // LANES
    dma = pltpu.SemaphoreType.DMA
    vm = pltpu.VMEM
    routes_t, scores_t = routes.T, route_scores.T
    wire = jax.ShapeDtypeStruct((slots * pieces, LANES), BF)
    sx, sg = pl.pallas_call(
        functools.partial(pre_kernel, n, cap),
        out_shape=(wire, wire),
        in_specs=[VMEM] * 4,
        out_specs=(VMEM, VMEM),
        scratch_shapes=[vm((slots * pieces, 128), F32)] * 2,
        name="pack",
    )(routes_t, scores_t, tokens, out_grad)
    block = (n, cap * pieces, LANES)
    share = width // (NX * NY)
    n_x = 3 * hidden // CHUNK - 1
    rows_x = width // NX
    rp, rg, ggu, gd = pl.pallas_call(
        functools.partial(expert_kernel, n, cap),
        out_shape=(
            jax.ShapeDtypeStruct(block, BF),
            jax.ShapeDtypeStruct(block, BF),
            jax.ShapeDtypeStruct((share, 2 * hidden), F32),
            jax.ShapeDtypeStruct((share, hidden), F32),
        ),
        in_specs=[ANY] * 4,
        out_specs=(ANY, ANY, VMEM, VMEM),
        scratch_shapes=[
            vm((width, 2 * hidden), BF), vm((width, hidden), BF),
            vm(block, BF), vm(block, BF),
            vm((slots * pieces, 128), F32), vm((slots * pieces, 128), F32),
            vm((slots, width), BF), vm((slots, width), BF),
            vm((slots, 2 * hidden), F32), vm((slots, hidden), BF), vm((slots, 2 * hidden), BF),
            vm(block, BF), vm(block, BF),
            vm((n_x, NX, rows_x, CHUNK), BF), vm((n_x, NX, rows_x, CHUNK), BF),
            vm((n_x, NY, share, CHUNK), BF), vm((n_x, NY, share, CHUNK), BF),
            vm((NX, NY, share, CHUNK), BF), vm((NY, NX, share, CHUNK), BF),
            vm((NX, share, CHUNK), BF), vm((NX, share, CHUNK), BF),
            dma((2,)), dma((2,)),
            dma((n,)), dma((n,)), dma((n,)), dma((n,)), dma((n,)), dma((n,)), dma((n,)), dma((n,)),
            dma((n_x, NX)), dma((n_x, NX)), dma((n_x, NY)), dma((n_x, NY)),
            dma((NY,)), dma((NY,)), dma((NX,)), dma((NX,)),
        ],
        compiler_params=pltpu.CompilerParams(
            collective_id=0, has_side_effects=True, vmem_limit_bytes=56 << 20
        ),
        name="experts",
    )(sx.reshape(block), sg.reshape(block), gate_up[0], down_weight[0])
    outs = jax.ShapeDtypeStruct((rows, width), BF)
    mixed, token_grad = pl.pallas_call(
        functools.partial(post_kernel, n, cap),
        out_shape=(outs, outs),
        in_specs=[VMEM] * 4,
        out_specs=(VMEM, VMEM),
        scratch_shapes=[vm((slots * pieces, 128), F32)] * 2,
        name="combine",
    )(routes_t, scores_t, rp.reshape(slots * pieces, LANES), rg.reshape(slots * pieces, LANES))
    return mixed, token_grad, ggu[None], gd[None]


def solution(mesh):
    in_specs = (
        P(("dp", "expert"), None),
        P(("dp", "expert"), None),
        P(("dp", "expert"), None),
        P(("dp", "expert"), None),
        P("expert", None, None),
        P("expert", None, None),
    )
    out_specs = (
        P(("dp", "expert"), None),
        P(("dp", "expert"), None),
        P("expert", "dp", None),
        P("expert", "dp", None),
    )
    return jax.shard_map(body, mesh=mesh, in_specs=in_specs, out_specs=out_specs, check_vma=False)
```

```python
import functools

import jax
import jax.numpy as jnp
from jax import lax
from jax.experimental import pallas as pl
from jax.experimental.pallas import tpu as pltpu
from jax.sharding import PartitionSpec as P

BF = jnp.bfloat16
F32 = jnp.float32
MESH = pl.DeviceIdType.MESH
NX, NY = 4, 8
LANES = 256
CHUNK = 256
VMEM = pl.BlockSpec(memory_space=pltpu.VMEM)
ANY = pl.BlockSpec(memory_space=pl.ANY)


def put(wide, j, pieces, value):
    rows = value.shape[0]
    for h in range(2):
        wide[h][pl.ds(j, rows, stride=pieces), :] = value[:, h * 128 : (h + 1) * 128]


def take(wide, j, pieces, rows):
    return jnp.concatenate([wide[h][pl.ds(j, rows, stride=pieces), :] for h in range(2)], axis=1)


def fill(wide, value):
    for h in range(2):
        wide[h][...] = value[:, h * 128 : (h + 1) * 128]


def whole(wide):
    return jnp.concatenate([wide[0][...], wide[1][...]], axis=1)


def dot(a, b, ca, cb):
    return lax.dot_general(a, b, (((ca,), (cb,)), ((), ())), preferred_element_type=F32)


def slots_of(routes, experts, cap):
    top, tokens = routes.shape
    ids = lax.broadcasted_iota(jnp.int32, (experts, tokens), 0)
    chosen = [(routes[k : k + 1, :] == ids).astype(F32) for k in range(top)]
    before = (
        lax.broadcasted_iota(jnp.int32, (tokens, tokens), 0)
        < lax.broadcasted_iota(jnp.int32, (tokens, tokens), 1)
    ).astype(F32)
    counts = dot(sum(chosen).astype(BF), before.astype(BF), 1, 0)
    return [
        routes[k : k + 1, :].astype(F32) * cap + jnp.sum(chosen[k] * counts, axis=0, keepdims=True)
        for k in range(top)
    ]


def route_weights(scores):
    e = jnp.exp(scores)
    return e / jnp.sum(e, axis=0, keepdims=True)


def token_kernel(slots, cols_ref, grad_ref, mixed_in, ggu_in, gd_in, mixed_ref, token_ref, ggu, gd, *wide):
    tokens, width = token_ref.shape
    pieces = width // LANES
    ids = lax.broadcasted_iota(jnp.int32, (tokens, slots), 1).astype(F32)
    cols = cols_ref[...]
    both = ((ids == cols[:, 2:3]) | (ids == cols[:, 3:4])).astype(F32).astype(BF)
    fill(wide, grad_ref[...].astype(F32))
    for j in range(pieces):
        part = take(wide, j, pieces, slots).astype(BF)
        token_ref[:, j * LANES : (j + 1) * LANES] = dot(both, part, 1, 0).astype(BF)
    mixed_ref[...] = mixed_in[...]
    ggu[...] = ggu_in[...]
    gd[...] = gd_in[...]


def expert_kernel(
    experts, cap, routes_ref, scores_ref, tokens_ref, grads_ref, win_hbm, wout_hbm, rg2, mixed, ggu, gd, cols,
    sx, sg, rp, win, wout, rx, rg, wide0, wide1, x, g, pre, hid, pg, s2p, s2g,
    ga, ra, y1, ry, gb, rb, x1, rx2,
    wsem, lsem, xs, xr, gs, gr, ps, pr, qs, qr, as_, ar, ys, yr, bs, br, cs, cr,
):
    wide = (wide0, wide1)
    me = lax.axis_index("expert")
    dp = lax.axis_index("dp")
    mx, my = dp // NY, lax.rem(dp, NY)
    n = experts
    slots = experts * cap
    width = x.shape[1]
    pieces = width // LANES
    hidden = hid.shape[1]
    n_in = 2 * hidden // CHUNK
    n_x = ga.shape[0]

    def zdev(k):
        return {"expert": lax.rem(me + k, n)}

    def xdev(d):
        return {"dp": lax.rem(mx + d, NX) * NY + my}

    def ydev(d):
        return {"dp": mx * NY + lax.rem(my + d, NY)}

    def remote(src, dst, ssem, rsem, dev):
        return pltpu.make_async_remote_copy(
            src_ref=src, dst_ref=dst, send_sem=ssem, recv_sem=rsem, device_id=dev, device_id_type=MESH
        )

    barrier = pltpu.get_barrier_semaphore()

    @pl.loop(1, n)
    def _(k):
        pl.semaphore_signal(barrier, inc=1, device_id=zdev(k), device_id_type=MESH)

    for d in range(1, NX):
        pl.semaphore_signal(barrier, inc=1, device_id=xdev(d), device_id_type=MESH)
    for d in range(1, NY):
        pl.semaphore_signal(barrier, inc=1, device_id=ydev(d), device_id_type=MESH)
    def dispatch(k, src, dst, ssem, rsem):
        return remote(src.at[lax.rem(me + k, n)], dst.at[k], ssem.at[k], rsem.at[k], zdev(k))

    def give_back(k, src, dst, ssem, rsem):
        return remote(src.at[k], dst.at[me], ssem.at[k], rsem.at[k], zdev(n - k))

    def start_all(make, *refs):
        @pl.loop(1, n // 2)
        def _(k):
            make(k, *refs).start()
            make(n - k, *refs).start()

        make(n // 2, *refs).start()

    def wait_sent(make, *refs):
        @pl.loop(1, n)
        def _(k):
            make(k, *refs).wait_send()

    own_x = pltpu.make_async_copy(sx.at[me], rx.at[0], lsem.at[0])
    own_g = pltpu.make_async_copy(sg.at[me], rg.at[0], lsem.at[1])
    load_in = pltpu.make_async_copy(win_hbm, win, wsem.at[0])
    load_out = pltpu.make_async_copy(wout_hbm, wout, wsem.at[1])
    load_in.start()
    load_out.start()

    slot0, slot1 = slots_of(routes_ref[...], n, cap)
    w = route_weights(scores_ref[...])
    ids = lax.broadcasted_iota(jnp.int32, (slots, w.shape[1]), 0).astype(F32)
    hot0, hot1 = (ids == slot0).astype(F32), (ids == slot1).astype(F32)
    slot_w = jnp.sum(hot0 * w[0:1, :] + hot1 * w[1:2, :], axis=1, keepdims=True)
    hot = (hot0 + hot1).astype(BF)
    cols[...] = jnp.transpose(jnp.concatenate([w, slot0, slot1, jnp.zeros((4, w.shape[1]), F32)], axis=0))

    def pack(src, dst, scale):
        for j in range(pieces):
            part = dot(hot, src[:, j * LANES : (j + 1) * LANES], 1, 0)
            put(wide, j, pieces, part if scale is None else part * scale)
        dst[...] = whole(wide).astype(BF).reshape(n, cap * pieces, LANES)

    pack(tokens_ref, sx, None)
    own_x.start()
    pl.semaphore_wait(barrier, (n - 1) + (NX - 1) + (NY - 1))
    start_all(dispatch, sx, rx, xs, xr)
    pack(grads_ref, sg, slot_w)
    own_g.start()
    start_all(dispatch, sg, rg, gs, gr)

    def narrow(src, dst):
        fill(wide, src[...].reshape(slots * pieces, LANES).astype(F32))
        for j in range(pieces):
            dst[:, j * LANES : (j + 1) * LANES] = take(wide, j, pieces, slots).astype(BF)

    def widen(rows, weights, dst):
        for j in range(pieces):
            put(wide, j, pieces, dot(rows, weights[j * LANES : (j + 1) * LANES, :], 1, 1))
        dst[...] = whole(wide).astype(BF).reshape(n, cap * pieces, LANES)

    own_x.wait()
    load_in.wait()
    load_out.wait()

    @pl.loop(1, n)
    def _(k):
        dispatch(k, sx, rx, xs, xr).wait_recv()

    narrow(rx, x)

    for c in range(hidden // CHUNK):
        lo, hi = c * CHUNK, (c + 1) * CHUNK
        gate = dot(x[...], win[:, lo:hi], 1, 0)
        up = dot(x[...], win[:, hidden + lo : hidden + hi], 1, 0)
        pre[:, lo:hi] = gate
        pre[:, hidden + lo : hidden + hi] = up
        hid[:, lo:hi] = (gate * (1.0 / (1.0 + jnp.exp(-gate))) * up).astype(BF)
    widen(hid[...], wout, s2p)
    start_all(give_back, s2p, rp, ps, pr)
    home_p = pltpu.make_async_copy(s2p.at[0], rp.at[me], lsem.at[0])
    home_p.start()

    own_g.wait()

    @pl.loop(1, n)
    def _(k):
        dispatch(k, sg, rg, gs, gr).wait_recv()

    narrow(rg, g)
    for c in range(hidden // CHUNK):
        lo, hi = c * CHUNK, (c + 1) * CHUNK
        hg = dot(g[...], wout[:, lo:hi], 1, 0)
        gate = pre[:, lo:hi]
        up = pre[:, hidden + lo : hidden + hi]
        s = 1.0 / (1.0 + jnp.exp(-gate))
        pg[:, lo:hi] = (hg * up * s * (1.0 + gate * (1.0 - s))).astype(BF)
        pg[:, hidden + lo : hidden + hi] = (hg * gate * s).astype(BF)

    rows_x = width // NX
    rows_y = rows_x // NY

    def send_a(c, d):
        return remote(
            ga.at[c, lax.rem(mx + d, NX)], ra.at[c, d], as_.at[c, d], ar.at[c, d], xdev(d)
        )

    def send_b(d):
        return remote(gb.at[:, lax.rem(my + d, NY)], rb.at[d], bs.at[d], br.at[d], ydev(d))

    def send_y(c, d):
        return remote(y1.at[c, lax.rem(my + d, NY)], ry.at[c, d], ys.at[c, d], yr.at[c, d], ydev(d))

    def send_c(d):
        return remote(x1.at[lax.rem(mx + d, NX)], rx2.at[d], cs.at[d], cr.at[d], xdev(d))

    last = hidden - CHUNK

    def piece_x(c):
        lo = c * CHUNK
        if c < n_in:
            part = dot(x[...], pg[:, lo : lo + CHUNK], 0, 0)
        else:
            lo -= n_in * CHUNK
            part = dot(g[...], hid[:, lo : lo + CHUNK], 0, 0)
        ga[c] = part.astype(BF).reshape(NX, rows_x, CHUNK)
        for d in (1, 3, 2):
            send_a(c, d).start()

    piece_x(0)
    gb[...] = dot(g[...], hid[:, last:hidden], 0, 0).astype(BF).reshape(NX, NY, rows_y, CHUNK)
    for d in (1, 7, 2, 6, 3, 5, 4):
        send_b(d).start()
    for c in range(1, n_x):
        piece_x(c)

    widen(pg[...], win, s2g)
    start_all(give_back, s2g, rg2, qs, qr)
    home_g = pltpu.make_async_copy(s2g.at[0], rg2.at[me], lsem.at[1])
    home_g.start()

    def sum_x(c):
        for d in range(1, NX):
            send_a(c, d).wait_recv()
        total = ga[c, mx].astype(F32)
        for d in range(1, NX):
            total = total + ra[c, d].astype(F32)
        y1[c] = total.astype(BF).reshape(NY, rows_y, CHUNK)
        for d in (1, 7, 2, 6, 3, 5, 4):
            send_y(c, d).start()

    def sum_y():
        for d in range(1, NY):
            send_b(d).wait_recv()
        total = gb[:, my].astype(F32)
        for d in range(1, NY):
            total = total + rb[d].astype(F32)
        x1[...] = total.astype(BF)
        for d in (1, 3, 2):
            send_c(d).start()

    def mix():
        home_p.wait()

        @pl.loop(1, n)
        def _(k):
            give_back(k, s2p, rp, ps, pr).wait_recv()

        mine = cols[...]
        tokens = mine.shape[0]
        at = lax.broadcasted_iota(jnp.int32, (tokens, slots), 1).astype(F32)
        first = (at == mine[:, 2:3]).astype(F32).astype(BF)
        second = (at == mine[:, 3:4]).astype(F32).astype(BF)
        fill(wide, rp[...].reshape(slots * pieces, LANES).astype(F32))
        for j in range(pieces):
            part = take(wide, j, pieces, slots).astype(BF)
            mixed[:, j * LANES : (j + 1) * LANES] = (
                mine[:, 0:1] * dot(first, part, 1, 0) + mine[:, 1:2] * dot(second, part, 1, 0)
            ).astype(BF)

    for c in range(n_x):
        sum_x(c)
        if c == 1:
            sum_y()
            mix()

    groups = float(NX * NY)
    for c in range(n_x):
        for d in range(1, NY):
            send_y(c, d).wait_recv()
        total = y1[c, my].astype(F32)
        for d in range(1, NY):
            total = total + ry[c, d].astype(F32)
        lo = c * CHUNK
        if c < n_in:
            ggu[:, lo : lo + CHUNK] = total / groups
        else:
            lo -= n_in * CHUNK
            gd[:, lo : lo + CHUNK] = total / groups
    for d in range(1, NX):
        send_c(d).wait_recv()
    total = x1[mx].astype(F32)
    for d in range(1, NX):
        total = total + rx2[d].astype(F32)
    gd[:, last:hidden] = total / groups

    home_g.wait()

    @pl.loop(1, n)
    def _(k):
        give_back(k, s2g, rg2, qs, qr).wait_recv()

    wait_sent(dispatch, sx, rx, xs, xr)
    wait_sent(dispatch, sg, rg, gs, gr)
    wait_sent(give_back, s2p, rp, ps, pr)
    wait_sent(give_back, s2g, rg2, qs, qr)
    for d in range(1, NX):
        for c in range(n_x):
            send_a(c, d).wait_send()
        send_c(d).wait_send()
    for d in range(1, NY):
        for c in range(n_x):
            send_y(c, d).wait_send()
        send_b(d).wait_send()


def body(tokens, routes, route_scores, out_grad, gate_up, down_weight):
    n = lax.axis_size("expert")
    rows, width = tokens.shape
    top = routes.shape[1]
    hidden = down_weight.shape[2]
    cap = (rows * top + n - 1) // n
    slots = n * cap
    pieces = width // LANES
    dma = pltpu.SemaphoreType.DMA
    vm = pltpu.VMEM
    block = (n, cap * pieces, LANES)
    share = width // (NX * NY)
    n_x = 3 * hidden // CHUNK - 1
    rows_x = width // NX
    outs = jax.ShapeDtypeStruct((rows, width), BF)
    shares = (
        jax.ShapeDtypeStruct((share, 2 * hidden), F32),
        jax.ShapeDtypeStruct((share, hidden), F32),
    )
    rg, mixed, ggu, gd, cols = pl.pallas_call(
        functools.partial(expert_kernel, n, cap),
        out_shape=(
            jax.ShapeDtypeStruct(block, BF),
            outs,
            *shares,
            jax.ShapeDtypeStruct((rows, 8), F32),
        ),
        in_specs=[VMEM] * 4 + [ANY] * 2,
        out_specs=(ANY, VMEM, VMEM, VMEM, VMEM),
        scratch_shapes=[
            vm(block, BF), vm(block, BF), vm(block, BF),
            vm((width, 2 * hidden), BF), vm((width, hidden), BF),
            vm(block, BF), vm(block, BF),
            vm((slots * pieces, 128), F32), vm((slots * pieces, 128), F32),
            vm((slots, width), BF), vm((slots, width), BF),
            vm((slots, 2 * hidden), F32), vm((slots, hidden), BF), vm((slots, 2 * hidden), BF),
            vm(block, BF), vm(block, BF),
            vm((n_x, NX, rows_x, CHUNK), BF), vm((n_x, NX, rows_x, CHUNK), BF),
            vm((n_x, NY, share, CHUNK), BF), vm((n_x, NY, share, CHUNK), BF),
            vm((NX, NY, share, CHUNK), BF), vm((NY, NX, share, CHUNK), BF),
            vm((NX, share, CHUNK), BF), vm((NX, share, CHUNK), BF),
            dma((2,)), dma((2,)),
            dma((n,)), dma((n,)), dma((n,)), dma((n,)), dma((n,)), dma((n,)), dma((n,)), dma((n,)),
            dma((n_x, NX)), dma((n_x, NX)), dma((n_x, NY)), dma((n_x, NY)),
            dma((NY,)), dma((NY,)), dma((NX,)), dma((NX,)),
        ],
        compiler_params=pltpu.CompilerParams(
            collective_id=0, has_side_effects=True, vmem_limit_bytes=56 << 20
        ),
        name="experts",
    )(routes.T, route_scores.T, tokens, out_grad, gate_up[0], down_weight[0])
    mixed, token_grad, ggu, gd = pl.pallas_call(
        functools.partial(token_kernel, slots),
        out_shape=(outs, outs, *shares),
        in_specs=[VMEM] * 5,
        out_specs=(VMEM,) * 4,
        scratch_shapes=[vm((slots * pieces, 128), F32)] * 2,
        name="token",
    )(cols, rg.reshape(slots * pieces, LANES), mixed, ggu, gd)
    return mixed, token_grad, ggu[None], gd[None]


def solution(mesh):
    in_specs = (
        P(("dp", "expert"), None),
        P(("dp", "expert"), None),
        P(("dp", "expert"), None),
        P(("dp", "expert"), None),
        P("expert", None, None),
        P("expert", None, None),
    )
    out_specs = (
        P(("dp", "expert"), None),
        P(("dp", "expert"), None),
        P("expert", "dp", None),
        P("expert", "dp", None),
    )
    return jax.shard_map(body, mesh=mesh, in_specs=in_specs, out_specs=out_specs, check_vma=False)
```

```python
import functools

import jax
import jax.numpy as jnp
from jax import lax
from jax.experimental import pallas as pl
from jax.experimental.pallas import tpu as pltpu
from jax.sharding import PartitionSpec as P

BF = jnp.bfloat16
F32 = jnp.float32
MESH = pl.DeviceIdType.MESH
NX, NY = 4, 8
LANES = 256
CHUNK = 256
VMEM = pl.BlockSpec(memory_space=pltpu.VMEM)
ANY = pl.BlockSpec(memory_space=pl.ANY)


def put(wide, j, pieces, value):
    rows = value.shape[0]
    for h in range(2):
        wide[h][pl.ds(j, rows, stride=pieces), :] = value[:, h * 128 : (h + 1) * 128]


def take(wide, j, pieces, rows):
    return jnp.concatenate([wide[h][pl.ds(j, rows, stride=pieces), :] for h in range(2)], axis=1)


def fill(wide, value):
    for h in range(2):
        wide[h][...] = value[:, h * 128 : (h + 1) * 128]


def whole(wide):
    return jnp.concatenate([wide[0][...], wide[1][...]], axis=1)


def dot(a, b, ca, cb):
    return lax.dot_general(a, b, (((ca,), (cb,)), ((), ())), preferred_element_type=F32)


def slots_of(routes, experts, cap):
    top, tokens = routes.shape
    ids = lax.broadcasted_iota(jnp.int32, (experts, tokens), 0)
    chosen = [(routes[k : k + 1, :] == ids).astype(F32) for k in range(top)]
    before = (
        lax.broadcasted_iota(jnp.int32, (tokens, tokens), 0)
        < lax.broadcasted_iota(jnp.int32, (tokens, tokens), 1)
    ).astype(F32)
    counts = dot(sum(chosen).astype(BF), before.astype(BF), 1, 0)
    return [
        routes[k : k + 1, :].astype(F32) * cap + jnp.sum(chosen[k] * counts, axis=0, keepdims=True)
        for k in range(top)
    ]


def route_weights(scores):
    e = jnp.exp(scores)
    return e / jnp.sum(e, axis=0, keepdims=True)


def token_kernel(slots, cols_ref, grad_ref, mixed_in, ggu_in, gd_in, mixed_ref, token_ref, ggu, gd, *wide):
    tokens, width = token_ref.shape
    pieces = width // LANES
    ids = lax.broadcasted_iota(jnp.int32, (tokens, slots), 1).astype(F32)
    cols = cols_ref[...]
    both = ((ids == cols[:, 2:3]) | (ids == cols[:, 3:4])).astype(F32).astype(BF)
    fill(wide, grad_ref[...].astype(F32))
    for j in range(pieces):
        part = take(wide, j, pieces, slots).astype(BF)
        token_ref[:, j * LANES : (j + 1) * LANES] = dot(both, part, 1, 0).astype(BF)
    mixed_ref[...] = mixed_in[...]
    ggu[...] = ggu_in[...]
    gd[...] = gd_in[...]


def expert_kernel(
    experts, cap, routes_hbm, scores_hbm, tokens_hbm, grads_hbm, win_hbm, wout_hbm, rg2, mixed_hbm, ggu_hbm, gd_hbm, cols_hbm,
    routes_ref, scores_ref, tokens_ref, grads_ref, mixed, ggu, gd, cols, isem, osem, sx, sg, rp, win, wout, rx, rg, wide0, wide1, x, g, pre, hid, pg, s2p, s2g,
    ga, ra, y1, ry, gb, rb, x1, rx2, rh,
    hs, hr, wsem, lsem, xs, xr, gs, gr, ps, pr, qs, qr, as_, ar, ys, yr, bs, br, cs, cr,
):
    wide = (wide0, wide1)
    me = lax.axis_index("expert")
    dp = lax.axis_index("dp")
    mx, my = dp // NY, lax.rem(dp, NY)
    n = experts
    slots = experts * cap
    width = x.shape[1]
    pieces = width // LANES
    hidden = hid.shape[1]
    n_in = 2 * hidden // CHUNK
    n_x = ga.shape[0]

    def zdev(k):
        return {"expert": lax.rem(me + k, n)}

    def xdev(d):
        return {"dp": lax.rem(mx + d, NX) * NY + my}

    def ydev(d):
        return {"dp": mx * NY + lax.rem(my + d, NY)}

    def remote(src, dst, ssem, rsem, dev):
        return pltpu.make_async_remote_copy(
            src_ref=src, dst_ref=dst, send_sem=ssem, recv_sem=rsem, device_id=dev, device_id_type=MESH
        )

    loads = [
        pltpu.make_async_copy(src, dst, isem.at[i])
        for i, (src, dst) in enumerate(
            (
                (routes_hbm, routes_ref),
                (scores_hbm, scores_ref),
                (tokens_hbm, tokens_ref),
                (grads_hbm, grads_ref),
            )
        )
    ]
    for load in loads:
        load.start()

    barrier = pltpu.get_barrier_semaphore()

    @pl.loop(1, n)
    def _(k):
        pl.semaphore_signal(barrier, inc=1, device_id=zdev(k), device_id_type=MESH)

    for d in range(1, NX):
        pl.semaphore_signal(barrier, inc=1, device_id=xdev(d), device_id_type=MESH)
    for d in range(1, NY):
        pl.semaphore_signal(barrier, inc=1, device_id=ydev(d), device_id_type=MESH)

    def dispatch(k, src, dst, ssem, rsem):
        return remote(src.at[lax.rem(me + k, n)], dst.at[k], ssem.at[k], rsem.at[k], zdev(k))

    def give_back(k, src, dst, ssem, rsem):
        return remote(src.at[k], dst.at[me], ssem.at[k], rsem.at[k], zdev(n - k))

    def start_all(make, *refs):
        @pl.loop(1, n // 2)
        def _(k):
            make(k, *refs).start()
            make(n - k, *refs).start()

        make(n // 2, *refs).start()

    def wait_sent(make, *refs):
        @pl.loop(1, n)
        def _(k):
            make(k, *refs).wait_send()

    own_x = pltpu.make_async_copy(sx.at[me], rx.at[0], lsem.at[0])
    own_g = pltpu.make_async_copy(sg.at[me], rg.at[0], lsem.at[1])
    load_in = pltpu.make_async_copy(win_hbm, win, wsem.at[0])
    load_out = pltpu.make_async_copy(wout_hbm, wout, wsem.at[1])
    load_in.start()
    load_out.start()

    loads[0].wait()
    loads[1].wait()
    slot0, slot1 = slots_of(routes_ref[...], n, cap)
    w = route_weights(scores_ref[...])
    ids = lax.broadcasted_iota(jnp.int32, (slots, w.shape[1]), 0).astype(F32)
    hot0, hot1 = (ids == slot0).astype(F32), (ids == slot1).astype(F32)
    slot_w = jnp.sum(hot0 * w[0:1, :] + hot1 * w[1:2, :], axis=1, keepdims=True)
    hot = (hot0 + hot1).astype(BF)
    cols[...] = jnp.transpose(jnp.concatenate([w, slot0, slot1, jnp.zeros((4, w.shape[1]), F32)], axis=0))

    def pack(src, dst, scale):
        for j in range(pieces):
            part = dot(hot, src[:, j * LANES : (j + 1) * LANES], 1, 0)
            put(wide, j, pieces, part if scale is None else part * scale)
        dst[...] = whole(wide).astype(BF).reshape(n, cap * pieces, LANES)

    loads[2].wait()
    pack(tokens_ref, sx, None)
    own_x.start()
    pl.semaphore_wait(barrier, (n - 1) + (NX - 1) + (NY - 1))
    start_all(dispatch, sx, rx, xs, xr)
    loads[3].wait()
    pack(grads_ref, sg, slot_w)
    own_g.start()
    start_all(dispatch, sg, rg, gs, gr)

    def narrow(src, dst):
        fill(wide, src[...].reshape(slots * pieces, LANES).astype(F32))
        for j in range(pieces):
            dst[:, j * LANES : (j + 1) * LANES] = take(wide, j, pieces, slots).astype(BF)

    def widen(rows, weights, dst):
        for j in range(pieces):
            put(wide, j, pieces, dot(rows, weights[j * LANES : (j + 1) * LANES, :], 1, 1))
        dst[...] = whole(wide).astype(BF).reshape(n, cap * pieces, LANES)

    outs = [
        pltpu.make_async_copy(src, dst, osem.at[i])
        for i, (src, dst) in enumerate(((mixed, mixed_hbm), (ggu, ggu_hbm), (gd, gd_hbm), (cols, cols_hbm)))
    ]
    outs[3].start()

    own_x.wait()
    load_in.wait()
    load_out.wait()

    @pl.loop(1, n)
    def _(k):
        dispatch(k, sx, rx, xs, xr).wait_recv()

    narrow(rx, x)

    for c in range(hidden // CHUNK):
        lo, hi = c * CHUNK, (c + 1) * CHUNK
        gate = dot(x[...], win[:, lo:hi], 1, 0)
        up = dot(x[...], win[:, hidden + lo : hidden + hi], 1, 0)
        pre[:, lo:hi] = gate
        pre[:, hidden + lo : hidden + hi] = up
        hid[:, lo:hi] = (gate * (1.0 / (1.0 + jnp.exp(-gate))) * up).astype(BF)
    widen(hid[...], wout, s2p)
    start_all(give_back, s2p, rp, ps, pr)
    home_p = pltpu.make_async_copy(s2p.at[0], rp.at[me], lsem.at[0])
    home_p.start()

    own_g.wait()

    @pl.loop(1, n)
    def _(k):
        dispatch(k, sg, rg, gs, gr).wait_recv()

    narrow(rg, g)
    for c in range(hidden // CHUNK):
        lo, hi = c * CHUNK, (c + 1) * CHUNK
        hg = dot(g[...], wout[:, lo:hi], 1, 0)
        gate = pre[:, lo:hi]
        up = pre[:, hidden + lo : hidden + hi]
        s = 1.0 / (1.0 + jnp.exp(-gate))
        pg[:, lo:hi] = (hg * up * s * (1.0 + gate * (1.0 - s))).astype(BF)
        pg[:, hidden + lo : hidden + hi] = (hg * gate * s).astype(BF)

    rows_x = width // NX
    rows_y = rows_x // NY

    def send_a(c, d):
        return remote(
            ga.at[c, lax.rem(mx + d, NX)], ra.at[c, d], as_.at[c, d], ar.at[c, d], xdev(d)
        )

    half = rows_x // 2
    near = (1, NX - 1)

    def send_h(c, d):
        return remote(
            ga.at[c, lax.rem(mx + 2, NX), pl.ds(d * half, half)], rh.at[c, d], hs.at[c, d], hr.at[c, d], xdev(near[d])
        )

    def relay(c):
        for d in range(2):
            send_h(c, d).wait_recv()
            block = lax.rem(mx + near[d], NX)
            rows = pl.ds(d * half, half)
            ga[c, block, rows] = (ga[c, block, rows].astype(F32) + rh[c, d].astype(F32)).astype(BF)
            send_a(c, near[d]).start()

    def send_b(d):
        return remote(gb.at[:, lax.rem(my + d, NY)], rb.at[d], bs.at[d], br.at[d], ydev(d))

    def send_y(c, d):
        return remote(y1.at[c, lax.rem(my + d, NY)], ry.at[c, d], ys.at[c, d], yr.at[c, d], ydev(d))

    def send_c(d):
        return remote(x1.at[lax.rem(mx + d, NX)], rx2.at[d], cs.at[d], cr.at[d], xdev(d))

    last = hidden - CHUNK

    def piece_x(c):
        lo = c * CHUNK
        if c < n_in:
            part = dot(x[...], pg[:, lo : lo + CHUNK], 0, 0)
        else:
            lo -= n_in * CHUNK
            part = dot(g[...], hid[:, lo : lo + CHUNK], 0, 0)
        ga[c] = part.astype(BF).reshape(NX, rows_x, CHUNK)
        for d in range(2):
            send_h(c, d).start()

    early = 2
    piece_x(0)
    gb[...] = dot(g[...], hid[:, last:hidden], 0, 0).astype(BF).reshape(NX, NY, rows_y, CHUNK)
    for d in (1, 7, 2, 6, 3, 5, 4):
        send_b(d).start()
    for c in range(1, n_x):
        piece_x(c)
        if c <= early:
            relay(c - 1)

    widen(pg[...], win, s2g)
    start_all(give_back, s2g, rg2, qs, qr)
    home_g = pltpu.make_async_copy(s2g.at[0], rg2.at[me], lsem.at[1])
    home_g.start()

    def sum_x(c):
        for d in near:
            send_a(c, d).wait_recv()
        total = ga[c, mx].astype(F32)
        for d in near:
            total = total + ra[c, d].astype(F32)
        y1[c] = total.astype(BF).reshape(NY, rows_y, CHUNK)
        for d in (1, 7, 2, 6, 3, 5, 4):
            send_y(c, d).start()

    def sum_y():
        for d in range(1, NY):
            send_b(d).wait_recv()
        total = gb[:, my].astype(F32)
        for d in range(1, NY):
            total = total + rb[d].astype(F32)
        x1[...] = total.astype(BF)
        for d in (1, 3, 2):
            send_c(d).start()

    def mix():
        home_p.wait()

        @pl.loop(1, n)
        def _(k):
            give_back(k, s2p, rp, ps, pr).wait_recv()

        mine = cols[...]
        tokens = mine.shape[0]
        at = lax.broadcasted_iota(jnp.int32, (tokens, slots), 1).astype(F32)
        first = (at == mine[:, 2:3]).astype(F32).astype(BF)
        second = (at == mine[:, 3:4]).astype(F32).astype(BF)
        fill(wide, rp[...].reshape(slots * pieces, LANES).astype(F32))
        for j in range(pieces):
            part = take(wide, j, pieces, slots).astype(BF)
            mixed[:, j * LANES : (j + 1) * LANES] = (
                mine[:, 0:1] * dot(first, part, 1, 0) + mine[:, 1:2] * dot(second, part, 1, 0)
            ).astype(BF)

    for c in range(early, n_x - 1):
        relay(c)
    for c in range(n_x):
        sum_x(c)
        if c == 0:
            relay(n_x - 1)
        if c == 1:
            sum_y()
            mix()
            outs[0].start()

    groups = float(NX * NY)
    for c in range(n_x):
        for d in range(1, NY):
            send_y(c, d).wait_recv()
        total = y1[c, my].astype(F32)
        for d in range(1, NY):
            total = total + ry[c, d].astype(F32)
        lo = c * CHUNK
        if c < n_in:
            ggu[:, lo : lo + CHUNK] = total / groups
        else:
            lo -= n_in * CHUNK
            gd[:, lo : lo + CHUNK] = total / groups
    for d in range(1, NX):
        send_c(d).wait_recv()
    total = x1[mx].astype(F32)
    for d in range(1, NX):
        total = total + rx2[d].astype(F32)
    gd[:, last:hidden] = total / groups
    outs[1].start()
    outs[2].start()

    home_g.wait()

    @pl.loop(1, n)
    def _(k):
        give_back(k, s2g, rg2, qs, qr).wait_recv()

    for out in outs:
        out.wait()
    wait_sent(dispatch, sx, rx, xs, xr)
    wait_sent(dispatch, sg, rg, gs, gr)
    wait_sent(give_back, s2p, rp, ps, pr)
    wait_sent(give_back, s2g, rg2, qs, qr)
    for d in range(1, NX):
        send_c(d).wait_send()
    for c in range(n_x):
        for d in range(2):
            send_h(c, d).wait_send()
            send_a(c, near[d]).wait_send()
    for d in range(1, NY):
        for c in range(n_x):
            send_y(c, d).wait_send()
        send_b(d).wait_send()


def body(tokens, routes, route_scores, out_grad, gate_up, down_weight):
    n = lax.axis_size("expert")
    rows, width = tokens.shape
    top = routes.shape[1]
    hidden = down_weight.shape[2]
    cap = (rows * top + n - 1) // n
    slots = n * cap
    pieces = width // LANES
    dma = pltpu.SemaphoreType.DMA
    vm = pltpu.VMEM
    block = (n, cap * pieces, LANES)
    share = width // (NX * NY)
    n_x = 3 * hidden // CHUNK - 1
    rows_x = width // NX
    outs = jax.ShapeDtypeStruct((rows, width), BF)
    shares = (
        jax.ShapeDtypeStruct((share, 2 * hidden), F32),
        jax.ShapeDtypeStruct((share, hidden), F32),
    )
    rg, mixed, ggu, gd, cols = pl.pallas_call(
        functools.partial(expert_kernel, n, cap),
        out_shape=(
            jax.ShapeDtypeStruct(block, BF),
            outs,
            *shares,
            jax.ShapeDtypeStruct((rows, 8), F32),
        ),
        in_specs=[ANY] * 6,
        out_specs=(ANY,) * 5,
        scratch_shapes=[
            vm((top, rows), jnp.int32), vm((top, rows), F32), vm((rows, width), BF), vm((rows, width), BF),
            vm((rows, width), BF), vm((share, 2 * hidden), F32), vm((share, hidden), F32), vm((rows, 8), F32),
            dma((4,)), dma((4,)),
            vm(block, BF), vm(block, BF), vm(block, BF),
            vm((width, 2 * hidden), BF), vm((width, hidden), BF),
            vm(block, BF), vm(block, BF),
            vm((slots * pieces, 128), F32), vm((slots * pieces, 128), F32),
            vm((slots, width), BF), vm((slots, width), BF),
            vm((slots, 2 * hidden), F32), vm((slots, hidden), BF), vm((slots, 2 * hidden), BF),
            vm(block, BF), vm(block, BF),
            vm((n_x, NX, rows_x, CHUNK), BF), vm((n_x, NX, rows_x, CHUNK), BF),
            vm((n_x, NY, share, CHUNK), BF), vm((n_x, NY, share, CHUNK), BF),
            vm((NX, NY, share, CHUNK), BF), vm((NY, NX, share, CHUNK), BF),
            vm((NX, share, CHUNK), BF), vm((NX, share, CHUNK), BF),
            vm((n_x, 2, rows_x // 2, CHUNK), BF),
            dma((n_x, 2)), dma((n_x, 2)),
            dma((2,)), dma((2,)),
            dma((n,)), dma((n,)), dma((n,)), dma((n,)), dma((n,)), dma((n,)), dma((n,)), dma((n,)),
            dma((n_x, NX)), dma((n_x, NX)), dma((n_x, NY)), dma((n_x, NY)),
            dma((NY,)), dma((NY,)), dma((NX,)), dma((NX,)),
        ],
        compiler_params=pltpu.CompilerParams(
            collective_id=0, has_side_effects=True, vmem_limit_bytes=56 << 20
        ),
        name="experts",
    )(routes.T, route_scores.T, tokens, out_grad, gate_up[0], down_weight[0])
    mixed, token_grad, ggu, gd = pl.pallas_call(
        functools.partial(token_kernel, slots),
        out_shape=(outs, outs, *shares),
        in_specs=[VMEM] * 5,
        out_specs=(VMEM,) * 4,
        scratch_shapes=[vm((slots * pieces, 128), F32)] * 2,
        name="token",
    )(cols, rg.reshape(slots * pieces, LANES), mixed, ggu, gd)
    return mixed, token_grad, ggu[None], gd[None]


def solution(mesh):
    in_specs = (
        P(("dp", "expert"), None),
        P(("dp", "expert"), None),
        P(("dp", "expert"), None),
        P(("dp", "expert"), None),
        P("expert", None, None),
        P("expert", None, None),
    )
    out_specs = (
        P(("dp", "expert"), None),
        P(("dp", "expert"), None),
        P("expert", "dp", None),
        P("expert", "dp", None),
    )
    return jax.shard_map(body, mesh=mesh, in_specs=in_specs, out_specs=out_specs, check_vma=False)
```

```python
import functools

import jax
import jax.numpy as jnp
from jax import lax
from jax.experimental import pallas as pl
from jax.experimental.pallas import tpu as pltpu
from jax.sharding import PartitionSpec as P

BF = jnp.bfloat16
F32 = jnp.float32
MESH = pl.DeviceIdType.MESH
NX, NY = 4, 8
LANES = 256
CHUNK = 256
VMEM = pl.BlockSpec(memory_space=pltpu.VMEM)
ANY = pl.BlockSpec(memory_space=pl.ANY)


def put(wide, j, pieces, value):
    rows = value.shape[0]
    for h in range(2):
        wide[h][pl.ds(j, rows, stride=pieces), :] = value[:, h * 128 : (h + 1) * 128]


def take(wide, j, pieces, rows):
    return jnp.concatenate([wide[h][pl.ds(j, rows, stride=pieces), :] for h in range(2)], axis=1)


def fill(wide, value):
    for h in range(2):
        wide[h][...] = value[:, h * 128 : (h + 1) * 128]


def whole(wide):
    return jnp.concatenate([wide[0][...], wide[1][...]], axis=1)


def dot(a, b, ca, cb):
    return lax.dot_general(a, b, (((ca,), (cb,)), ((), ())), preferred_element_type=F32)


def slots_of(routes, experts, cap):
    top, tokens = routes.shape
    ids = lax.broadcasted_iota(jnp.int32, (experts, tokens), 0)
    chosen = [(routes[k : k + 1, :] == ids).astype(F32) for k in range(top)]
    before = (
        lax.broadcasted_iota(jnp.int32, (tokens, tokens), 0)
        < lax.broadcasted_iota(jnp.int32, (tokens, tokens), 1)
    ).astype(F32)
    counts = dot(sum(chosen).astype(BF), before.astype(BF), 1, 0)
    return [
        routes[k : k + 1, :].astype(F32) * cap + jnp.sum(chosen[k] * counts, axis=0, keepdims=True)
        for k in range(top)
    ]


def route_weights(scores):
    e = jnp.exp(scores)
    return e / jnp.sum(e, axis=0, keepdims=True)


def token_kernel(slots, cols_ref, grad_ref, mixed_in, ggu_in, gd_in, mixed_ref, token_ref, ggu, gd, *wide):
    tokens, width = token_ref.shape
    pieces = width // LANES
    ids = lax.broadcasted_iota(jnp.int32, (tokens, slots), 1).astype(F32)
    cols = cols_ref[...]
    both = ((ids == cols[:, 2:3]) | (ids == cols[:, 3:4])).astype(F32).astype(BF)
    fill(wide, grad_ref[...].astype(F32))
    for j in range(pieces):
        part = take(wide, j, pieces, slots).astype(BF)
        token_ref[:, j * LANES : (j + 1) * LANES] = dot(both, part, 1, 0).astype(BF)
    mixed_ref[...] = mixed_in[...]
    ggu[...] = ggu_in[...]
    gd[...] = gd_in[...]


def expert_kernel(
    experts, cap, routes_hbm, scores_hbm, tokens_hbm, grads_hbm, win_hbm, wout_hbm, rg2, mixed_hbm, ggu_hbm, gd_hbm, cols_hbm,
    routes_ref, scores_ref, tokens_ref, grads_ref, mixed, ggu, gd, cols, isem, osem, sx, sg, rp, win, wout, rx, rg, wide0, wide1, x, g, pre, hid, pg, s2p, s2g,
    ga, ra, y1, ry, gb, rb, x1, rx2, rh,
    hs, hr, wsem, lsem, xs, xr, gs, gr, ps, pr, qs, qr, as_, ar, ys, yr, bs, br, cs, cr,
):
    wide = (wide0, wide1)
    me = lax.axis_index("expert")
    dp = lax.axis_index("dp")
    mx, my = dp // NY, lax.rem(dp, NY)
    n = experts
    slots = experts * cap
    width = x.shape[1]
    pieces = width // LANES
    hidden = hid.shape[1]
    n_in = 2 * hidden // CHUNK
    n_x = ga.shape[0]

    def zdev(k):
        return {"expert": lax.rem(me + k, n)}

    def xdev(d):
        return {"dp": lax.rem(mx + d, NX) * NY + my}

    def ydev(d):
        return {"dp": mx * NY + lax.rem(my + d, NY)}

    def remote(src, dst, ssem, rsem, dev):
        return pltpu.make_async_remote_copy(
            src_ref=src, dst_ref=dst, send_sem=ssem, recv_sem=rsem, device_id=dev, device_id_type=MESH
        )

    loads = [
        pltpu.make_async_copy(src, dst, isem.at[i])
        for i, (src, dst) in enumerate(
            (
                (routes_hbm, routes_ref),
                (scores_hbm, scores_ref),
                (tokens_hbm, tokens_ref),
                (grads_hbm, grads_ref),
            )
        )
    ]
    for load in loads:
        load.start()

    barrier = pltpu.get_barrier_semaphore()

    @pl.loop(1, n)
    def _(k):
        pl.semaphore_signal(barrier, inc=1, device_id=zdev(k), device_id_type=MESH)

    for d in range(1, NX):
        pl.semaphore_signal(barrier, inc=1, device_id=xdev(d), device_id_type=MESH)
    for d in range(1, NY):
        pl.semaphore_signal(barrier, inc=1, device_id=ydev(d), device_id_type=MESH)

    third = n // 3
    ahead = third // 2

    def dispatch(k, src, dst, ssem, rsem):
        return remote(src.at[lax.rem(k + ahead, n)], dst.at[k], ssem.at[k], rsem.at[k], zdev(k))

    def give_back(k, src, dst, ssem, rsem):
        return remote(src.at[k], dst.at[me], ssem.at[k], rsem.at[k], zdev(n - k))

    def start_all(make, *refs):
        @pl.loop(1, n // 2)
        def _(k):
            make(k, *refs).start()
            make(n - k, *refs).start()

        make(n // 2, *refs).start()

    def wait_sent(make, *refs):
        @pl.loop(1, n)
        def _(k):
            make(k, *refs).wait_send()

    own_x = pltpu.make_async_copy(sx.at[ahead], rx.at[0], lsem.at[0])
    own_g = pltpu.make_async_copy(sg.at[ahead], rg.at[0], lsem.at[1])
    load_in = pltpu.make_async_copy(win_hbm, win, wsem.at[0])
    load_out = pltpu.make_async_copy(wout_hbm, wout, wsem.at[1])
    load_in.start()
    load_out.start()

    loads[0].wait()
    loads[1].wait()
    slot0, slot1 = slots_of(routes_ref[...], n, cap)
    w = route_weights(scores_ref[...])
    ids = lax.broadcasted_iota(jnp.int32, (slots, w.shape[1]), 0).astype(F32)
    turn = (lax.rem(n - me + ahead, n) * cap).astype(F32)

    def turned(slot):
        slot = slot + turn
        return jnp.where(slot >= slots, slot - slots, slot)

    hot0, hot1 = (ids == turned(slot0)).astype(F32), (ids == turned(slot1)).astype(F32)
    slot_w = jnp.sum(hot0 * w[0:1, :] + hot1 * w[1:2, :], axis=1, keepdims=True)
    hot = hot0 + hot1
    cols[...] = jnp.transpose(jnp.concatenate([w, slot0, slot1, jnp.zeros((4, w.shape[1]), F32)], axis=0))

    def pack(src, dst, scale, lo, blocks):
        first, rows = lo * cap, blocks * cap
        pick = hot[first : first + rows].astype(BF)
        for j in range(pieces):
            part = dot(pick, src[:, j * LANES : (j + 1) * LANES], 1, 0)
            put(wide, first * pieces + j, pieces, part if scale is None else part * scale)
        wire = pl.ds(first * pieces, rows * pieces)
        packed = jnp.concatenate([wide[h][wire, :] for h in range(2)], axis=1).astype(BF)
        dst[lo : lo + blocks] = packed.reshape(blocks, cap * pieces, LANES)

    loads[2].wait()
    pack(tokens_ref, sx, None, 0, third)
    own_x.start()
    pl.semaphore_wait(barrier, (n - 1) + (NX - 1) + (NY - 1))
    for part in range(3):
        if part:
            pack(tokens_ref, sx, None, part * third, third)
        away = [i - ahead for i in range(part * third, (part + 1) * third)]
        for k in sorted((k for k in away if k), key=lambda k: min(k % n, -k % n)):
            dispatch(k % n, sx, rx, xs, xr).start()
    loads[3].wait()
    pack(grads_ref, sg, slot_w, 0, n)
    own_g.start()
    start_all(dispatch, sg, rg, gs, gr)

    def narrow(src, dst):
        fill(wide, src[...].reshape(slots * pieces, LANES).astype(F32))
        for j in range(pieces):
            dst[:, j * LANES : (j + 1) * LANES] = take(wide, j, pieces, slots).astype(BF)

    def widen(rows, weights, dst):
        for j in range(pieces):
            put(wide, j, pieces, dot(rows, weights[j * LANES : (j + 1) * LANES, :], 1, 1))
        dst[...] = whole(wide).astype(BF).reshape(n, cap * pieces, LANES)

    outs = [
        pltpu.make_async_copy(src, dst, osem.at[i])
        for i, (src, dst) in enumerate(((mixed, mixed_hbm), (ggu, ggu_hbm), (gd, gd_hbm), (cols, cols_hbm)))
    ]
    outs[3].start()

    own_x.wait()
    load_in.wait()
    load_out.wait()

    @pl.loop(1, n)
    def _(k):
        dispatch(k, sx, rx, xs, xr).wait_recv()

    narrow(rx, x)

    for c in range(hidden // CHUNK):
        lo, hi = c * CHUNK, (c + 1) * CHUNK
        gate = dot(x[...], win[:, lo:hi], 1, 0)
        up = dot(x[...], win[:, hidden + lo : hidden + hi], 1, 0)
        pre[:, lo:hi] = gate
        pre[:, hidden + lo : hidden + hi] = up
        hid[:, lo:hi] = (gate * (1.0 / (1.0 + jnp.exp(-gate))) * up).astype(BF)
    widen(hid[...], wout, s2p)
    start_all(give_back, s2p, rp, ps, pr)
    home_p = pltpu.make_async_copy(s2p.at[0], rp.at[me], lsem.at[0])
    home_p.start()

    own_g.wait()

    @pl.loop(1, n)
    def _(k):
        dispatch(k, sg, rg, gs, gr).wait_recv()

    narrow(rg, g)
    for c in range(hidden // CHUNK):
        lo, hi = c * CHUNK, (c + 1) * CHUNK
        hg = dot(g[...], wout[:, lo:hi], 1, 0)
        gate = pre[:, lo:hi]
        up = pre[:, hidden + lo : hidden + hi]
        s = 1.0 / (1.0 + jnp.exp(-gate))
        pg[:, lo:hi] = (hg * up * s * (1.0 + gate * (1.0 - s))).astype(BF)
        pg[:, hidden + lo : hidden + hi] = (hg * gate * s).astype(BF)

    rows_x = width // NX
    rows_y = rows_x // NY

    def send_a(c, d):
        return remote(
            ga.at[c, lax.rem(mx + d, NX)], ra.at[c, d], as_.at[c, d], ar.at[c, d], xdev(d)
        )

    half = rows_x // 2
    near = (1, NX - 1)

    def send_h(c, d):
        return remote(
            ga.at[c, lax.rem(mx + 2, NX), pl.ds(d * half, half)], rh.at[c, d], hs.at[c, d], hr.at[c, d], xdev(near[d])
        )

    def relay(c):
        for d in range(2):
            send_h(c, d).wait_recv()
            block = lax.rem(mx + near[d], NX)
            rows = pl.ds(d * half, half)
            ga[c, block, rows] = (ga[c, block, rows].astype(F32) + rh[c, d].astype(F32)).astype(BF)
            send_a(c, near[d]).start()

    def send_b(d):
        return remote(gb.at[:, lax.rem(my + d, NY)], rb.at[d], bs.at[d], br.at[d], ydev(d))

    def send_y(c, d):
        return remote(y1.at[c, lax.rem(my + d, NY)], ry.at[c, d], ys.at[c, d], yr.at[c, d], ydev(d))

    def send_c(d):
        return remote(x1.at[lax.rem(mx + d, NX)], rx2.at[d], cs.at[d], cr.at[d], xdev(d))

    last = hidden - CHUNK

    def piece_x(c):
        lo = c * CHUNK
        if c < n_in:
            part = dot(x[...], pg[:, lo : lo + CHUNK], 0, 0)
        else:
            lo -= n_in * CHUNK
            part = dot(g[...], hid[:, lo : lo + CHUNK], 0, 0)
        ga[c] = part.astype(BF).reshape(NX, rows_x, CHUNK)
        for d in range(2):
            send_h(c, d).start()

    early = 2
    piece_x(0)
    gb[...] = dot(g[...], hid[:, last:hidden], 0, 0).astype(BF).reshape(NX, NY, rows_y, CHUNK)
    for d in (1, 7, 2, 6, 3, 5, 4):
        send_b(d).start()
    for c in range(1, n_x):
        piece_x(c)
        if c <= early:
            relay(c - 1)

    widen(pg[...], win, s2g)
    give_back(n // 2, s2g, rg2, qs, qr).start()

    @pl.loop(1, n // 2)
    def _(k):
        give_back(n // 2 - k, s2g, rg2, qs, qr).start()
        give_back(n // 2 + k, s2g, rg2, qs, qr).start()

    home_g = pltpu.make_async_copy(s2g.at[0], rg2.at[me], lsem.at[1])
    home_g.start()

    def sum_x(c):
        for d in near:
            send_a(c, d).wait_recv()
        total = ga[c, mx].astype(F32)
        for d in near:
            total = total + ra[c, d].astype(F32)
        y1[c] = total.astype(BF).reshape(NY, rows_y, CHUNK)
        for d in (1, 7, 2, 6, 3, 5, 4):
            send_y(c, d).start()

    def sum_y():
        for d in range(1, NY):
            send_b(d).wait_recv()
        total = gb[:, my].astype(F32)
        for d in range(1, NY):
            total = total + rb[d].astype(F32)
        x1[...] = total.astype(BF)
        for d in (1, 3, 2):
            send_c(d).start()

    def mix():
        home_p.wait()

        @pl.loop(1, n)
        def _(k):
            give_back(k, s2p, rp, ps, pr).wait_recv()

        mine = cols[...]
        tokens = mine.shape[0]
        at = lax.broadcasted_iota(jnp.int32, (tokens, slots), 1).astype(F32)
        first = (at == mine[:, 2:3]).astype(F32).astype(BF)
        second = (at == mine[:, 3:4]).astype(F32).astype(BF)
        fill(wide, rp[...].reshape(slots * pieces, LANES).astype(F32))
        for j in range(pieces):
            part = take(wide, j, pieces, slots).astype(BF)
            mixed[:, j * LANES : (j + 1) * LANES] = (
                mine[:, 0:1] * dot(first, part, 1, 0) + mine[:, 1:2] * dot(second, part, 1, 0)
            ).astype(BF)

    for c in range(early, n_x - 1):
        relay(c)
    for c in range(n_x):
        sum_x(c)
        if c == 0:
            relay(n_x - 1)
        if c == 1:
            sum_y()
            mix()
            outs[0].start()

    groups = float(NX * NY)
    for c in range(n_x):
        for d in range(1, NY):
            send_y(c, d).wait_recv()
        total = y1[c, my].astype(F32)
        for d in range(1, NY):
            total = total + ry[c, d].astype(F32)
        lo = c * CHUNK
        if c < n_in:
            ggu[:, lo : lo + CHUNK] = total / groups
        else:
            lo -= n_in * CHUNK
            gd[:, lo : lo + CHUNK] = total / groups
    for d in range(1, NX):
        send_c(d).wait_recv()
    total = x1[mx].astype(F32)
    for d in range(1, NX):
        total = total + rx2[d].astype(F32)
    gd[:, last:hidden] = total / groups
    outs[1].start()
    outs[2].start()

    home_g.wait()

    @pl.loop(1, n)
    def _(k):
        give_back(k, s2g, rg2, qs, qr).wait_recv()

    for out in outs:
        out.wait()
    wait_sent(dispatch, sx, rx, xs, xr)
    wait_sent(dispatch, sg, rg, gs, gr)
    wait_sent(give_back, s2p, rp, ps, pr)
    wait_sent(give_back, s2g, rg2, qs, qr)
    for d in range(1, NX):
        send_c(d).wait_send()
    for c in range(n_x):
        for d in range(2):
            send_h(c, d).wait_send()
            send_a(c, near[d]).wait_send()
    for d in range(1, NY):
        for c in range(n_x):
            send_y(c, d).wait_send()
        send_b(d).wait_send()


def body(tokens, routes, route_scores, out_grad, gate_up, down_weight):
    n = lax.axis_size("expert")
    rows, width = tokens.shape
    top = routes.shape[1]
    hidden = down_weight.shape[2]
    cap = (rows * top + n - 1) // n
    slots = n * cap
    pieces = width // LANES
    dma = pltpu.SemaphoreType.DMA
    vm = pltpu.VMEM
    block = (n, cap * pieces, LANES)
    share = width // (NX * NY)
    n_x = 3 * hidden // CHUNK - 1
    rows_x = width // NX
    outs = jax.ShapeDtypeStruct((rows, width), BF)
    shares = (
        jax.ShapeDtypeStruct((share, 2 * hidden), F32),
        jax.ShapeDtypeStruct((share, hidden), F32),
    )
    rg, mixed, ggu, gd, cols = pl.pallas_call(
        functools.partial(expert_kernel, n, cap),
        out_shape=(
            jax.ShapeDtypeStruct(block, BF),
            outs,
            *shares,
            jax.ShapeDtypeStruct((rows, 8), F32),
        ),
        in_specs=[ANY] * 6,
        out_specs=(ANY,) * 5,
        scratch_shapes=[
            vm((top, rows), jnp.int32), vm((top, rows), F32), vm((rows, width), BF), vm((rows, width), BF),
            vm((rows, width), BF), vm((share, 2 * hidden), F32), vm((share, hidden), F32), vm((rows, 8), F32),
            dma((4,)), dma((4,)),
            vm(block, BF), vm(block, BF), vm(block, BF),
            vm((width, 2 * hidden), BF), vm((width, hidden), BF),
            vm(block, BF), vm(block, BF),
            vm((slots * pieces, 128), F32), vm((slots * pieces, 128), F32),
            vm((slots, width), BF), vm((slots, width), BF),
            vm((slots, 2 * hidden), F32), vm((slots, hidden), BF), vm((slots, 2 * hidden), BF),
            vm(block, BF), vm(block, BF),
            vm((n_x, NX, rows_x, CHUNK), BF), vm((n_x, NX, rows_x, CHUNK), BF),
            vm((n_x, NY, share, CHUNK), BF), vm((n_x, NY, share, CHUNK), BF),
            vm((NX, NY, share, CHUNK), BF), vm((NY, NX, share, CHUNK), BF),
            vm((NX, share, CHUNK), BF), vm((NX, share, CHUNK), BF),
            vm((n_x, 2, rows_x // 2, CHUNK), BF),
            dma((n_x, 2)), dma((n_x, 2)),
            dma((2,)), dma((2,)),
            dma((n,)), dma((n,)), dma((n,)), dma((n,)), dma((n,)), dma((n,)), dma((n,)), dma((n,)),
            dma((n_x, NX)), dma((n_x, NX)), dma((n_x, NY)), dma((n_x, NY)),
            dma((NY,)), dma((NY,)), dma((NX,)), dma((NX,)),
        ],
        compiler_params=pltpu.CompilerParams(
            collective_id=0, has_side_effects=True, vmem_limit_bytes=56 << 20
        ),
        name="experts",
    )(routes.T, route_scores.T, tokens, out_grad, gate_up[0], down_weight[0])
    mixed, token_grad, ggu, gd = pl.pallas_call(
        functools.partial(token_kernel, slots),
        out_shape=(outs, outs, *shares),
        in_specs=[VMEM] * 5,
        out_specs=(VMEM,) * 4,
        scratch_shapes=[vm((slots * pieces, 128), F32)] * 2,
        name="token",
    )(cols, rg.reshape(slots * pieces, LANES), mixed, ggu, gd)
    return mixed, token_grad, ggu[None], gd[None]


def solution(mesh):
    in_specs = (
        P(("dp", "expert"), None),
        P(("dp", "expert"), None),
        P(("dp", "expert"), None),
        P(("dp", "expert"), None),
        P("expert", None, None),
        P("expert", None, None),
    )
    out_specs = (
        P(("dp", "expert"), None),
        P(("dp", "expert"), None),
        P("expert", "dp", None),
        P("expert", "dp", None),
    )
    return jax.shard_map(body, mesh=mesh, in_specs=in_specs, out_specs=out_specs, check_vma=False)
```
